512 devices in a mesh: seq: 16 (over y, x), mp: 32 (over z, core).
Axes of the slice: x: 4, y: 4, z: 16, core: 2. Of those that a mesh axis runs over, the one named last changes fastest.
Arguments:
- q_proj: bfloat16 [4096, 8192], P('seq', 'mp'), may hold values from -6 to 6
- k_proj: bfloat16 [4096, 8192], P('seq', 'mp'), may hold values from -6 to 6
- v_proj: bfloat16 [4096, 8192], P('seq', 'mp'), may hold values from -6 to 6
- out_grad: bfloat16 [4096, 8192], P('seq', 'mp'), may hold values from -0.75 to 0.75
- out_weight: bfloat16 [8192, 8192], P('mp', 'seq'), may hold values from -0.0625 to 0.0625
- taps: float32 [7, 512], P(None, 'mp'), may hold values from -2.4 to 2.4
Outputs:
- grad_q: bfloat16 [4096, 8192], P('seq', 'mp')
- grad_k: bfloat16 [4096, 8192], P('seq', 'mp')
- grad_v: bfloat16 [4096, 8192], P('seq', 'mp')
- grad_weight: float32 [8192, 8192], P('mp', 'seq')
- grad_taps: float32 [7, 512], P(None, 'mp')
The draws below stay inside these ranges and needn't reach their ends.
All inputs are finite; a program needn't handle non-finite values.
Results may differ from the reference program's by a relative error of at most 0.0029.
Values may be sent and summed in bfloat16 or wider, within the bound.
A program may use at most 64 MiB of HBM per device.

```python
import jax
import jax.numpy as jnp

D = 8192
TAPS = 7
GROUP = 16
LENGTH = 4096
FILTERS = 512


def block_scale(own_key, dims, split, least, top_value):
    factor_of, own = 1.0, jax.random.fold_in(own_key, 6)
    for dim, parts in split:
        heights = jnp.exp(jax.random.uniform(jax.random.fold_in(own, dim), (parts,), jnp.float32, least / len(split), top_value / len(split)))
        factor_of = factor_of * jnp.repeat(heights, dims[dim] // parts).reshape([-1 if axis == dim else 1 for axis in range(len(dims))])
    return factor_of


def bell_draw(key, shape, width, most, pieces=(), held_as=jnp.bfloat16):
    gain = block_scale(key, shape, pieces, -0.22, 0.18) if pieces else 1.0
    drawn = jax.random.normal(key, shape, jnp.float32) * width * gain
    return jnp.minimum(jnp.maximum(drawn, -most), most).astype(held_as)


def setup_inputs(seed: int = 0) -> dict:
    arg_keys = jax.random.split(jax.random.key(seed), 7)
    return {
        "q_proj": bell_draw(arg_keys[0], (LENGTH, D), 1.0, 6.0, ((0, 16), (1, 32))),
        "k_proj": bell_draw(arg_keys[1], (LENGTH, D), 1.0, 6.0, ((0, 16), (1, 32))),
        "v_proj": bell_draw(arg_keys[2], (LENGTH, D), 1.0, 6.0, ((0, 16), (1, 32))),
        "out_grad": bell_draw(arg_keys[3], (LENGTH, D), 0.125, 0.75, ((0, 16), (1, 32))),
        "out_weight": bell_draw(arg_keys[4], (D, D), D ** -0.5, 0.0625, ((0, 32), (1, 16))),
        "taps": bell_draw(arg_keys[5], (TAPS, FILTERS), 0.4, 2.4, ((1, 32),), jnp.float32),
    }


def reference(q_proj, k_proj, v_proj, out_grad, out_weight, taps):
    length, channels = q_proj.shape
    rim_rows = TAPS - 1
    q_full = q_proj.astype(jnp.float32)
    k_full = k_proj.astype(jnp.float32)
    v_full = v_proj.astype(jnp.float32)
    spread = jnp.repeat(taps, GROUP, axis=1)
    product = jnp.concatenate([jnp.zeros((rim_rows, channels), jnp.float32), k_full * v_full], 0)
    filtered = jnp.zeros((length, channels), jnp.float32)
    for offset in range(TAPS):
        filtered = filtered + spread[offset] * product[rim_rows - offset:rim_rows - offset + length]
    gated = (q_full * filtered).astype(jnp.bfloat16)
    grad_gated = jnp.dot(out_grad, out_weight.T, preferred_element_type=jnp.float32)
    grad_weight = jnp.dot(gated.T, out_grad, preferred_element_type=jnp.float32)
    grad_q = (grad_gated * filtered).astype(jnp.bfloat16)
    grad_filtered = grad_gated * q_full
    grad_ext = jnp.concatenate([grad_filtered, jnp.zeros((rim_rows, channels), jnp.float32)], 0)
    grad_product = jnp.zeros((length, channels), jnp.float32)
    for offset in range(TAPS):
        grad_product = grad_product + spread[offset] * grad_ext[offset:offset + length]
    grad_k = (grad_product * v_full).astype(jnp.bfloat16)
    grad_v = (grad_product * k_full).astype(jnp.bfloat16)
    filter_terms = jnp.stack([jnp.sum(grad_filtered * product[rim_rows - offset:rim_rows - offset + length], 0) for offset in range(TAPS)])
    grad_taps = filter_terms.reshape(TAPS, channels // GROUP, GROUP).sum(-1)
    return (grad_q, grad_k, grad_v, grad_weight, grad_taps)
```

```python
import jax
import jax.numpy as jnp
from jax import lax
from jax.sharding import PartitionSpec as P

TAPS = 7
GROUP = 16


def passed_along(array, axis, by):
    count = lax.axis_size(axis)
    pairs = [(i, i + by) for i in range(count) if 0 <= i + by < count]
    return lax.ppermute(array, axis, pairs)


def shards(q_proj, k_proj, v_proj, out_grad, out_weight, taps):
    tokens, channels = q_proj.shape
    rim_rows = TAPS - 1
    q_full = q_proj.astype(jnp.float32)
    k_full = k_proj.astype(jnp.float32)
    v_full = v_proj.astype(jnp.float32)
    spread = jnp.broadcast_to(taps[:, :, None], (TAPS, taps.shape[1], GROUP)).reshape(
        TAPS, channels
    )
    tail_rows = jnp.stack([k_proj[tokens - rim_rows :], v_proj[tokens - rim_rows :]])
    before = passed_along(tail_rows, "seq", 1)
    keys_wide = jnp.concatenate([before[0], k_proj], 0).astype(jnp.float32)
    values_wide = jnp.concatenate([before[1], v_proj], 0).astype(jnp.float32)
    product = keys_wide * values_wide
    filtered = jnp.zeros((tokens, channels), jnp.float32)
    for offset in range(TAPS):
        filtered = (
            filtered + spread[offset] * product[rim_rows - offset : rim_rows - offset + tokens]
        )
    gated = (q_full * filtered).astype(jnp.bfloat16)
    seq_count, mp_count = lax.axis_size("seq"), lax.axis_size("mp")
    cores = mp_count // seq_count
    pairs = [
        (t * mp_count + cores * z + c, z * mp_count + cores * t + c)
        for t in range(seq_count)
        for z in range(seq_count)
        for c in range(cores)
    ]
    crossed = lax.ppermute(out_grad, ("seq", "mp"), pairs)
    tiles = lax.all_gather(crossed, "mp", axis=0)
    columns = (
        tiles.reshape(seq_count, cores, tokens, channels)
        .transpose(0, 2, 1, 3)
        .reshape(seq_count * tokens, cores * channels)
    )
    partial = lax.dot_general(
        columns, out_weight, (((1,), (1,)), ((), ())), preferred_element_type=jnp.float32
    )
    grad_gated = lax.psum_scatter(partial, "seq", scatter_dimension=0, tiled=True)
    grad_weight = lax.dot_general(
        lax.all_gather(gated, "seq", axis=0, tiled=True),
        columns,
        (((0,), (0,)), ((), ())),
        preferred_element_type=jnp.float32,
    )
    grad_q = (grad_gated * filtered).astype(jnp.bfloat16)
    grad_filtered = grad_gated * q_full
    following = passed_along(grad_filtered[:rim_rows], "seq", -1)
    grad_ext = jnp.concatenate([grad_filtered, following], 0)
    grad_product = jnp.zeros((tokens, channels), jnp.float32)
    for offset in range(TAPS):
        grad_product = grad_product + spread[offset] * grad_ext[offset : offset + tokens]
    grad_k = (grad_product * v_full).astype(jnp.bfloat16)
    grad_v = (grad_product * k_full).astype(jnp.bfloat16)
    filter_terms = jnp.stack(
        [
            jnp.sum(grad_filtered * product[rim_rows - offset : rim_rows - offset + tokens], 0)
            for offset in range(TAPS)
        ]
    )
    filter_local = filter_terms.reshape(TAPS, channels // GROUP, GROUP).sum(-1)
    grad_taps = lax.psum(filter_local, "seq")
    return (grad_q, grad_k, grad_v, grad_weight, grad_taps)


def solution(mesh):
    placed = (
        P("seq", "mp"),
        P("seq", "mp"),
        P("seq", "mp"),
        P("seq", "mp"),
        P("mp", "seq"),
        P(None, "mp"),
    )
    return jax.shard_map(
        shards,
        mesh=mesh,
        in_specs=placed,
        out_specs=(P("seq", "mp"), P("seq", "mp"), P("seq", "mp"), P("mp", "seq"), P(None, "mp")),
        check_vma=False,
    )
```

```python
import functools

import jax
import jax.numpy as jnp
from jax import lax
from jax.experimental import pallas as pl
from jax.experimental.pallas import tpu as pltpu
from jax.sharding import PartitionSpec as P

TAPS = 7
GROUP = 16
PAD = 16
EDGE = 8
MESH = pl.DeviceIdType.MESH
F32 = jnp.float32
BF16 = jnp.bfloat16


def dot(a, b, dims):
    return lax.dot_general(a, b, ((dims[0:1], dims[1:2]), ((), ())), preferred_element_type=F32)


def exact_dot(a, b):
    return lax.dot_general(
        a,
        b,
        (((1,), (0,)), ((), ())),
        precision=lax.Precision.HIGHEST,
        preferred_element_type=F32,
    )


def kernel(
    side,
    q_ref, k_ref, v_ref, g_ref, w_ref, taps_ref,
    gq_ref, gk_ref, gv_ref, gw_ref, gt_ref,
    cols, gat, sent1, got1, own, sent2, got2, fin,
    k_edge, v_edge, prod, filt, gfil, spread, terms, terms_got,
    cross_s, cross_r, cross_l, edge_s, edge_r, ga_s, ga_r, gb_s, gb_r,
    ring_s, ring_r, core_s, core_r, one_s, one_r, two_s, two_r,
    back_s, back_r, term_s, term_r,
):
    n = side * side
    far = n // 2
    rows, chans = q_ref.shape
    half, wide = rows // 2, chans // 2
    s, m = lax.axis_index("seq"), lax.axis_index("mp")
    z, c = m // 2, m % 2
    y, x = s // side, s % side

    def ring(t):
        return lax.rem(t + 2 * n, n)

    def seq_dev(i):
        return (i, m)

    def at_xy(yy, xx):
        return (lax.rem(yy + side, side) * side + lax.rem(xx + side, side), m)

    def rc(src, dst, ss, rs, dev):
        return pltpu.make_async_remote_copy(
            src_ref=src, dst_ref=dst, send_sem=ss, recv_sem=rs, device_id=dev, device_id_type=MESH
        )

    crossed = (z, 2 * s + c)
    up, down = (s, 2 * ring(z + 1) + c), (s, 2 * ring(z - 1) + c)
    mate = (s, 2 * z + 1 - c)
    off_diagonal = s != z

    barrier = pltpu.get_barrier_semaphore()
    for d in range(1, n):
        pl.semaphore_signal(
            barrier, inc=1, device_id=seq_dev(ring(s + d)), device_id_type=MESH
        )
    for dev in (up, down, mate):
        pl.semaphore_signal(barrier, inc=1, device_id=dev, device_id_type=MESH)

    @pl.when(off_diagonal)
    def _():
        pl.semaphore_signal(barrier, inc=1, device_id=crossed, device_id_type=MESH)
        pl.semaphore_wait(barrier, n + 3)

    @pl.when(jnp.logical_not(off_diagonal))
    def _():
        pl.semaphore_wait(barrier, n + 2)

    def cross():
        return rc(g_ref, cols.at[c, s], cross_s.at[0], cross_r.at[0], crossed)

    def cross_in():
        return rc(g_ref, cols.at[c, z], cross_s.at[0], cross_r.at[0], crossed)

    def cross_local():
        return pltpu.make_async_copy(g_ref, cols.at[c, z], cross_l.at[0])

    @pl.when(off_diagonal)
    def _():
        cross().start()

    @pl.when(jnp.logical_not(off_diagonal))
    def _():
        cross_local().start()

    def edges(dev):
        tail = pl.ds(rows - PAD, PAD)
        return (
            rc(k_ref.at[tail], k_edge, edge_s.at[0], edge_r.at[0], seq_dev(dev)),
            rc(v_ref.at[tail], v_edge, edge_s.at[1], edge_r.at[1], seq_dev(dev)),
        )

    @pl.when(s < n - 1)
    def _():
        for copy in edges(s + 1):
            copy.start()

    group = lax.broadcasted_iota(jnp.int32, (GROUP, chans), 1) // GROUP
    lane = lax.broadcasted_iota(jnp.int32, (GROUP, chans), 0)
    spread[0:TAPS] = exact_dot(taps_ref[...], jnp.where(group == lane, 1.0, 0.0).astype(F32))
    prod[PAD:] = k_ref[...].astype(F32) * v_ref[...].astype(F32)

    @pl.when(s == 0)
    def _():
        prod[0:PAD] = jnp.zeros((PAD, chans), F32)

    @pl.when(s > 0)
    def _():
        for copy in edges(s - 1):
            copy.wait_recv()
        prod[0:PAD] = k_edge[...].astype(F32) * v_edge[...].astype(F32)

    total = jnp.zeros((rows, chans), F32)
    for o in range(TAPS):
        total = total + spread[o : o + 1] * prod[PAD - o : PAD - o + rows]
    filt[...] = total
    gated = (q_ref[...].astype(F32) * total).astype(BF16)
    gat[s, 0] = gated[:half]
    gat[s, 1] = gated[half:]

    def gather_a(h, d, sign):
        to = at_xy(y, x + d * sign) if h == 0 else at_xy(y + d * sign, x)
        block = s if sign > 0 else to[0]
        piece = gat.at[block, h]
        return rc(piece, piece, ga_s.at[h, d - 1], ga_r.at[h, d - 1], to)

    def gather_b(h, d, e, sign):
        if h == 0:
            block, to = at_xy(y, x - e)[0], at_xy(y + d * sign, x)
            came = at_xy(y - d, x - e)[0]
        else:
            block, to = at_xy(y - e, x)[0], at_xy(y, x + d * sign)
            came = at_xy(y - e, x - d)[0]
        piece = gat.at[block if sign > 0 else came, h]
        return rc(piece, piece, gb_s.at[h, d - 1, e], gb_r.at[h, d - 1, e], to)

    for d in range(1, side):
        for h in range(2):
            gather_a(h, d, 1).start()
    for h in range(2):
        for d in range(1, side):
            gather_b(h, d, 0, 1).start()
    for e in range(1, side):
        for h in range(2):
            gather_a(h, e, -1).wait_recv()
            for d in range(1, side):
                gather_b(h, d, e, 1).start()

    def hop(way, k, j, t):
        piece = cols.at[c, t, pl.ds(j * half, half)]
        sems = ring_s.at[way, k, j], ring_r.at[way, k, j]
        return rc(piece, piece, *sems, up if way == 0 else down)

    def share(t, which):
        piece = cols.at[which, t]
        return rc(piece, piece, core_s.at[t], core_r.at[t], mate)

    gw_ref[...] = jnp.zeros(gw_ref.shape, F32)

    @pl.when(off_diagonal)
    def _():
        cross_in().wait_recv()

    @pl.when(jnp.logical_not(off_diagonal))
    def _():
        cross_local().wait()

    for j in range(2):
        for way in range(2):
            if far > 1 or way == j:
                hop(way, 0, j, z).start()
    share(z, c).start()
    for h in range(2):
        for d in range(1, side):
            for e in range(side):
                gather_b(h, d, e, -1).wait_recv()

    def leg_one(h, t):
        ty, tx = t // side, t % side
        outer, inner, here = (ty, tx, x) if h == 0 else (tx, ty, y)
        d = lax.rem(inner - here + side, side)
        to = at_xy(y, tx) if h == 0 else at_xy(ty, x)
        return outer, d, to

    def one_copy(h, t, outer, d, to):
        return rc(
            sent1.at[h, t], got1.at[h, outer, d - 1],
            one_s.at[h, outer, d - 1], one_r.at[h, outer, d - 1], to,
        )

    def process(t):
        share(t, 1 - c).wait_recv()
        left, right = cols[0, t], cols[1, t]
        part = dot(left, w_ref[:, :chans], (1, 1)) + dot(right, w_ref[:, chans:], (1, 1))
        for h in range(2):
            outer, d, to = leg_one(h, t)
            piece = part[:, h * wide : (h + 1) * wide]

            @pl.when(d == 0)
            def _():
                own[h, outer] = piece

            @pl.when(d != 0)
            def _():
                sent1[h, t] = piece.astype(BF16)
                one_copy(h, t, outer, d, to).start()

        for j in range(2):
            near = gat[t, j]
            span = slice(j * half, (j + 1) * half)
            gw_ref[:, :chans] += dot(near, left[span], (0, 0))
            gw_ref[:, chans:] += dot(near, right[span], (0, 0))

    def leg_two(h, t):
        ty, tx = t // side, t % side
        outer, there = (ty, y) if h == 0 else (tx, x)
        d = lax.rem(outer - there + side, side)
        to = at_xy(ty, x) if h == 0 else at_xy(y, tx)
        return outer, d, to

    def two_copy(h, outer, d, to):
        return rc(
            sent2.at[h, outer], got2.at[h, d - 1], two_s.at[h, d - 1], two_r.at[h, d - 1], to
        )

    def finish(t):
        for h in range(2):
            _, d_one, _ = leg_one(h, t)
            outer, d, to = leg_two(h, t)

            @pl.when(d_one == 0)
            def _():
                acc = own[h, outer]
                for e in range(1, side):
                    one_copy(h, t, outer, e, at_xy(y, x - 1)).wait_recv()
                    acc = acc + got1[h, outer, e - 1].astype(F32)

                @pl.when(d == 0)
                def _():
                    fin[h] = acc

                @pl.when(d != 0)
                def _():
                    sent2[h, outer] = acc
                    two_copy(h, outer, d, to).start()

    def step(k, carry):
        a, b = ring(z - k), ring(z + k)

        @pl.when(k < far)
        def _():
            for j in range(2):
                for way, t in ((0, a), (1, b)):
                    hop(way, k - 1, j, t).wait_recv()
                    if way == j:
                        hop(way, k, j, t).start()
                    else:

                        @pl.when(k < far - 1)
                        def _():
                            hop(way, k, j, t).start()

            share(a, c).start()
            share(b, c).start()

        @pl.when(k == far)
        def _():
            for way in range(2):
                hop(way, far - 1, way, a).wait_recv()
            share(a, c).start()

        @pl.when(k <= far + 1)
        def _():
            process(ring(z - k + 1))

        @pl.when(jnp.logical_and(k > 1, k <= far))
        def _():
            process(ring(z + k - 1))

        @pl.when(k >= 3)
        def _():
            finish(ring(z - k + 3))

        @pl.when(jnp.logical_and(k > 3, k <= far + 2))
        def _():
            finish(ring(z + k - 3))

        return carry

    lax.fori_loop(1, far + 4, step, 0)

    for h in range(2):
        span = slice(h * wide, (h + 1) * wide)
        acc = fin[h]
        for d in range(1, side):
            two_copy(h, 0, d, at_xy(y, x - 1)).wait_recv()
            acc = acc + got2[h, d - 1]
        gq_ref[:, span] = (acc * filt[:, span]).astype(BF16)
        gfil[0:rows, span] = acc * q_ref[:, span].astype(F32)

    def back(dev):
        return rc(
            gfil.at[pl.ds(0, EDGE)], gfil.at[pl.ds(rows, EDGE)],
            back_s.at[0], back_r.at[0], seq_dev(dev),
        )

    @pl.when(s > 0)
    def _():
        back(s - 1).start()

    @pl.when(s == n - 1)
    def _():
        gfil[rows:] = jnp.zeros((EDGE, chans), F32)

    grad_filtered = gfil[0:rows]
    term_rows = [
        jnp.sum(grad_filtered * prod[PAD - o : PAD - o + rows], 0, keepdims=True)
        for o in range(TAPS)
    ]
    stacked = jnp.concatenate(term_rows + [jnp.zeros((1, chans), F32)], 0)
    lanes = terms.shape[1]
    group_t = lax.broadcasted_iota(jnp.int32, (chans, lanes), 0) // GROUP
    lane_t = lax.broadcasted_iota(jnp.int32, (chans, lanes), 1)
    terms[...] = exact_dot(stacked, jnp.where(group_t == lane_t, 1.0, 0.0).astype(F32))

    def term(d, dev):
        return rc(terms, terms_got.at[d - 1], term_s.at[d - 1], term_r.at[d - 1], seq_dev(dev))

    for d in range(1, n):
        term(d, ring(s + d)).start()

    @pl.when(s < n - 1)
    def _():
        back(s + 1).wait_recv()

    grad_product = jnp.zeros((rows, chans), F32)
    for o in range(TAPS):
        grad_product = grad_product + spread[o : o + 1] * gfil[o : o + rows]
    gk_ref[...] = (grad_product * v_ref[...].astype(F32)).astype(BF16)
    gv_ref[...] = (grad_product * k_ref[...].astype(F32)).astype(BF16)

    term_sum = terms[...]
    for d in range(1, n):
        term(d, ring(s - d)).wait_recv()
        term_sum = term_sum + terms_got[d - 1]
    gt_ref[...] = term_sum[0:TAPS, 0:GROUP]

    @pl.when(off_diagonal)
    def _():
        cross().wait_send()

    @pl.when(s < n - 1)
    def _():
        for copy in edges(s + 1):
            copy.wait_send()

    for h in range(2):
        for d in range(1, side):
            gather_a(h, d, 1).wait_send()
            for e in range(side):
                gather_b(h, d, e, 1).wait_send()

    def sent_hops(k, carry):
        for j in range(2):
            for way in range(2):
                if way == j:
                    hop(way, k, j, z).wait_send()
                else:

                    @pl.when(k < far - 1)
                    def _():
                        hop(way, k, j, z).wait_send()

        return carry

    lax.fori_loop(0, far, sent_hops, 0)

    def sent_shares(t, carry):
        share(t, c).wait_send()
        return carry

    lax.fori_loop(0, n, sent_shares, 0)

    def sent_sums(outer, carry):
        for h in range(2):
            for d in range(1, side):
                one_copy(h, 0, outer, d, at_xy(y, x - 1)).wait_send()
        return carry

    lax.fori_loop(0, side, sent_sums, 0)
    for h in range(2):
        for d in range(1, side):
            two_copy(h, 0, d, at_xy(y, x - 1)).wait_send()

    @pl.when(s > 0)
    def _():
        back(s - 1).wait_send()

    for d in range(1, n):
        term(d, ring(s + d)).wait_send()


def shards(side, q, k, v, g, w, taps):
    n = side * side
    rows, chans = q.shape
    half, wide = rows // 2, chans // 2
    vmem = pl.BlockSpec(memory_space=pltpu.VMEM)
    dma = pltpu.SemaphoreType.DMA
    sems = [
        (1,), (1,), (1,), (2,), (2,),
        (2, side - 1), (2, side - 1), (2, side - 1, side), (2, side - 1, side),
        (2, n // 2, 2), (2, n // 2, 2), (n,), (n,),
        (2, side, side - 1), (2, side, side - 1), (2, side - 1), (2, side - 1),
        (1,), (1,), (n - 1,), (n - 1,),
    ]
    return pl.pallas_call(
        functools.partial(kernel, side),
        out_shape=(
            jax.ShapeDtypeStruct((rows, chans), BF16),
            jax.ShapeDtypeStruct((rows, chans), BF16),
            jax.ShapeDtypeStruct((rows, chans), BF16),
            jax.ShapeDtypeStruct(w.shape, F32),
            jax.ShapeDtypeStruct(taps.shape, F32),
        ),
        in_specs=[vmem] * 6,
        out_specs=[vmem] * 5,
        scratch_shapes=[
            pltpu.VMEM((2, n, rows, chans), BF16),
            pltpu.VMEM((n, 2, half, chans), BF16),
            pltpu.VMEM((2, n, rows, wide), BF16),
            pltpu.VMEM((2, side, side - 1, rows, wide), BF16),
            pltpu.VMEM((2, side, rows, wide), F32),
            pltpu.VMEM((2, side, rows, wide), F32),
            pltpu.VMEM((2, side - 1, rows, wide), F32),
            pltpu.VMEM((2, rows, wide), F32),
            pltpu.VMEM((PAD, chans), BF16),
            pltpu.VMEM((PAD, chans), BF16),
            pltpu.VMEM((PAD + rows, chans), F32),
            pltpu.VMEM((rows, chans), F32),
            pltpu.VMEM((rows + EDGE, chans), F32),
            pltpu.VMEM((8, chans), F32),
            pltpu.VMEM((8, 128), F32),
            pltpu.VMEM((n - 1, 8, 128), F32),
        ]
        + [dma(shape) for shape in sems],
        compiler_params=pltpu.CompilerParams(
            collective_id=0, has_side_effects=True, vmem_limit_bytes=48 * 2**20
        ),
    )(q, k, v, g, w, taps)


def solution(mesh):
    side = int(round(mesh.shape["seq"] ** 0.5))
    tiles, weight, filters = P("seq", "mp"), P("mp", "seq"), P(None, "mp")
    return jax.shard_map(
        functools.partial(shards, side),
        mesh=mesh,
        in_specs=(tiles, tiles, tiles, tiles, weight, filters),
        out_specs=(tiles, tiles, tiles, weight, filters),
        check_vma=False,
    )
```

```python
import functools

import jax
import jax.numpy as jnp
from jax import lax
from jax.experimental import pallas as pl
from jax.experimental.pallas import tpu as pltpu
from jax.sharding import PartitionSpec as P

TAPS = 7
GROUP = 16
PAD = 16
EDGE = 8
PARTS = 4
MESH = pl.DeviceIdType.MESH
F32 = jnp.float32
BF16 = jnp.bfloat16


def dot(a, b, dims):
    return lax.dot_general(a, b, ((dims[0:1], dims[1:2]), ((), ())), preferred_element_type=F32)


def exact_dot(a, b):
    return lax.dot_general(
        a,
        b,
        (((1,), (0,)), ((), ())),
        precision=lax.Precision.HIGHEST,
        preferred_element_type=F32,
    )


def kernel(
    side,
    q_in, k_in, v_in, g_ref, w_in, taps_in,
    gq_ref, gk_ref, gv_ref, gw_ref, gt_ref,
    cols, gat, sent1, got1, own, sent2, got2, fin,
    q_ref, k_ref, v_ref, w_ref, taps_ref, k_edge, v_edge, prod, filt, gfil, spread, terms, terms_got,
    cross_s, cross_r, cross_l, edge_s, edge_r, ga_s, ga_r, gb_s, gb_r,
    ring_s, ring_r, core_s, core_r, one_s, one_r, two_s, two_r,
    back_s, back_r, term_s, term_r, load_s,
):
    n = side * side
    far = n // 2
    rows, chans = q_in.shape
    half, wide, slab = rows // 2, chans // 2, rows // PARTS
    s, m = lax.axis_index("seq"), lax.axis_index("mp")
    z, c = m // 2, m % 2
    y, x = s // side, s % side
    loads = [
        pltpu.make_async_copy(src, dst, load_s.at[i])
        for i, (src, dst) in enumerate(
            ((k_in, k_ref), (v_in, v_ref), (taps_in, taps_ref), (q_in, q_ref), (w_in, w_ref))
        )
    ]
    for load in loads:
        load.start()

    def ring(t):
        return lax.rem(t + 4 * n, n)

    def seq_dev(i):
        return (i, m)

    def at_xy(yy, xx):
        return (lax.rem(yy + side, side) * side + lax.rem(xx + side, side), m)

    def rc(src, dst, ss, rs, dev):
        return pltpu.make_async_remote_copy(
            src_ref=src, dst_ref=dst, send_sem=ss, recv_sem=rs, device_id=dev, device_id_type=MESH
        )


    def skew(i):
        return i + side * (i % side)

    target = ring(s + skew(z))
    crossed = (z, 2 * target + c)
    source = (ring(z - skew(s)), 2 * s + c)
    up, down = (s, 2 * ring(z + 1) + c), (s, 2 * ring(z - 1) + c)
    mate = (s, 2 * z + 1 - c)
    off_diagonal = jnp.logical_or(s != z, target != z)

    barrier = pltpu.get_barrier_semaphore()
    for d in range(1, n):
        pl.semaphore_signal(
            barrier, inc=1, device_id=seq_dev(ring(s + d)), device_id_type=MESH
        )
    for dev in (up, down, mate):
        pl.semaphore_signal(barrier, inc=1, device_id=dev, device_id_type=MESH)

    @pl.when(off_diagonal)
    def _():
        pl.semaphore_signal(barrier, inc=1, device_id=source, device_id_type=MESH)
        pl.semaphore_wait(barrier, n + 3)

    @pl.when(jnp.logical_not(off_diagonal))
    def _():
        pl.semaphore_wait(barrier, n + 2)

    def cross():
        return rc(g_ref, cols.at[c, target], cross_s.at[0], cross_r.at[0], crossed)

    def cross_in():
        return rc(g_ref, cols.at[c, z], cross_s.at[0], cross_r.at[0], crossed)

    def cross_local():
        return pltpu.make_async_copy(g_ref, cols.at[c, z], cross_l.at[0])

    @pl.when(off_diagonal)
    def _():
        cross().start()

    @pl.when(jnp.logical_not(off_diagonal))
    def _():
        cross_local().start()

    def edges(dev):
        tail = pl.ds(rows - PAD, PAD)
        return (
            rc(k_in.at[tail], k_edge, edge_s.at[0], edge_r.at[0], seq_dev(dev)),
            rc(v_in.at[tail], v_edge, edge_s.at[1], edge_r.at[1], seq_dev(dev)),
        )

    @pl.when(s < n - 1)
    def _():
        for copy in edges(s + 1):
            copy.start()

    for load in loads:
        load.wait()
    group = lax.broadcasted_iota(jnp.int32, (GROUP, chans), 1) // GROUP
    lane = lax.broadcasted_iota(jnp.int32, (GROUP, chans), 0)
    spread[0:TAPS] = exact_dot(taps_ref[...], jnp.where(group == lane, 1.0, 0.0).astype(F32))
    prod[PAD:] = k_ref[...].astype(F32) * v_ref[...].astype(F32)

    @pl.when(s == 0)
    def _():
        prod[0:PAD] = jnp.zeros((PAD, chans), F32)

    @pl.when(s > 0)
    def _():
        for copy in edges(s - 1):
            copy.wait_recv()
        prod[0:PAD] = k_edge[...].astype(F32) * v_edge[...].astype(F32)

    total = jnp.zeros((rows, chans), F32)
    for o in range(TAPS):
        total = total + spread[o : o + 1] * prod[PAD - o : PAD - o + rows]
    filt[...] = total
    gated = (q_ref[...].astype(F32) * total).astype(BF16)
    gat[s] = gated

    def gather_a(h, d, sign):
        to = at_xy(y, x + d * sign) if h == 0 else at_xy(y + d * sign, x)
        block = s if sign > 0 else to[0]
        piece = gat.at[block, pl.ds(h * half, half)]
        return rc(piece, piece, ga_s.at[h, d - 1], ga_r.at[h, d - 1], to)

    def gather_b(h, d, e, sign):
        if h == 0:
            block, to = at_xy(y, x - e)[0], at_xy(y + d * sign, x)
            came = at_xy(y - d, x - e)[0]
        else:
            block, to = at_xy(y - e, x)[0], at_xy(y, x + d * sign)
            came = at_xy(y - e, x - d)[0]
        piece = gat.at[block if sign > 0 else came, pl.ds(h * half, half)]
        return rc(piece, piece, gb_s.at[h, d - 1, e], gb_r.at[h, d - 1, e], to)

    for d in range(1, side):
        for h in range(2):
            gather_a(h, d, 1).start()
    for h in range(2):
        for d in range(1, side):
            gather_b(h, d, 0, 1).start()
    for e in range(1, side):
        for h in range(2):
            gather_a(h, e, -1).wait_recv()
            for d in range(1, side):
                gather_b(h, d, e, 1).start()

    def hop(way, k, j, t):
        piece = cols.at[c, t, pl.ds(j * slab, slab)]
        sems = ring_s.at[way, k, j], ring_r.at[way, k, j]
        return rc(piece, piece, *sems, up if way == 0 else down)

    def share(t, which):
        piece = cols.at[which, t]
        return rc(piece, piece, core_s.at[t], core_r.at[t], mate)

    @pl.when(off_diagonal)
    def _():
        cross_in().wait_recv()

    @pl.when(jnp.logical_not(off_diagonal))
    def _():
        cross_local().wait()

    for j in range(PARTS):
        for way in range(2):
            hop(way, 0, j, z).start()
    share(z, c).start()

    def last_way(j):
        return 2 * j // PARTS

    def leg_one(h, t):
        ty, tx = t // side, t % side
        outer, inner, here = (ty, tx, x) if h == 0 else (tx, ty, y)
        d = lax.rem(inner - here + side, side)
        to = at_xy(y, tx) if h == 0 else at_xy(ty, x)
        return outer, d, to

    def one_copy(h, t, outer, d, to):
        return rc(
            sent1.at[h, t], got1.at[h, outer, d - 1],
            one_s.at[h, outer, d - 1], one_r.at[h, outer, d - 1], to,
        )

    def process(p):
        t = ring(p - skew(s))
        share(p, 1 - c).wait_recv()
        part = dot(cols[0, p], w_ref[:, :chans], (1, 1)) + dot(cols[1, p], w_ref[:, chans:], (1, 1))
        for h in range(2):
            outer, d, to = leg_one(h, t)
            piece = part[:, h * wide : (h + 1) * wide]

            @pl.when(d == 0)
            def _():
                own[h, outer] = piece

            @pl.when(d != 0)
            def _():
                sent1[h, t] = piece.astype(BF16)
                one_copy(h, t, outer, d, to).start()

    def two_copy(h, outer, d, to):
        return rc(
            sent2.at[h, outer], got2.at[h, d - 1], two_s.at[h, d - 1], two_r.at[h, d - 1], to
        )

    def step(k, carry):
        a, b = ring(z - k), ring(z + k)

        def pass_on(j):
            @pl.when(k < far)
            def _():
                for way, p in ((0, a), (1, b)):
                    hop(way, k - 1, j, p).wait_recv()
                    if way == last_way(j):
                        hop(way, k, j, p).start()
                    else:

                        @pl.when(k < far - 1)
                        def _():
                            hop(way, k, j, p).start()

            @pl.when(k == far)
            def _():
                hop(last_way(j), far - 1, j, a).wait_recv()

        for j in range(PARTS // 2):
            pass_on(j)
        process(ring(z - k + 1))
        for j in range(PARTS // 2, PARTS):
            pass_on(j)

        @pl.when(k <= far)
        def _():
            share(a, c).start()

        @pl.when(k < far)
        def _():
            share(b, c).start()

        @pl.when(jnp.logical_and(k > 1, k <= far))
        def _():
            process(ring(z + k - 1))

        return carry

    lax.fori_loop(1, far + 2, step, 0)

    for i in range(1, side + 1):
        d = i % side
        for h in range(2):
            outer = lax.rem((y if h == 0 else x) + i, side)
            acc = own[h, outer]
            for e in range(1, side):
                one_copy(h, 0, outer, e, at_xy(y, x - 1)).wait_recv()
                acc = acc + got1[h, outer, e - 1].astype(F32)
            if d:
                sent2[h, outer] = acc
                two_copy(h, outer, d, at_xy(y + d, x) if h == 0 else at_xy(y, x + d)).start()
            else:
                fin[h] = acc

    for h in range(2):
        for d in range(1, side):
            for e in range(side):
                gather_b(h, d, e, -1).wait_recv()
    gw_ref[...] = jnp.zeros(gw_ref.shape, F32)

    def weigh(p, carry):
        near = gat[ring(p - skew(s))]
        gw_ref[:, :chans] += dot(near, cols[0, p], (0, 0))
        gw_ref[:, chans:] += dot(near, cols[1, p], (0, 0))
        return carry

    lax.fori_loop(0, n, weigh, 0)

    for h in range(2):
        span = slice(h * wide, (h + 1) * wide)
        acc = fin[h]
        for d in range(1, side):
            two_copy(h, 0, d, at_xy(y, x - 1)).wait_recv()
            acc = acc + got2[h, d - 1]
        gq_ref[:, span] = (acc * filt[:, span]).astype(BF16)
        gfil[0:rows, span] = acc * q_ref[:, span].astype(F32)

    def back(dev):
        return rc(
            gfil.at[pl.ds(0, EDGE)], gfil.at[pl.ds(rows, EDGE)],
            back_s.at[0], back_r.at[0], seq_dev(dev),
        )

    @pl.when(s > 0)
    def _():
        back(s - 1).start()

    @pl.when(s == n - 1)
    def _():
        gfil[rows:] = jnp.zeros((EDGE, chans), F32)

    grad_filtered = gfil[0:rows]
    term_rows = [
        jnp.sum(grad_filtered * prod[PAD - o : PAD - o + rows], 0, keepdims=True)
        for o in range(TAPS)
    ]
    stacked = jnp.concatenate(term_rows + [jnp.zeros((1, chans), F32)], 0)
    lanes = terms.shape[1]
    group_t = lax.broadcasted_iota(jnp.int32, (chans, lanes), 0) // GROUP
    lane_t = lax.broadcasted_iota(jnp.int32, (chans, lanes), 1)
    terms[...] = exact_dot(stacked, jnp.where(group_t == lane_t, 1.0, 0.0).astype(F32))

    def term(d, dev):
        return rc(terms, terms_got.at[d - 1], term_s.at[d - 1], term_r.at[d - 1], seq_dev(dev))

    for d in range(1, n):
        term(d, ring(s + d)).start()

    @pl.when(s < n - 1)
    def _():
        back(s + 1).wait_recv()

    grad_product = jnp.zeros((rows, chans), F32)
    for o in range(TAPS):
        grad_product = grad_product + spread[o : o + 1] * gfil[o : o + rows]
    gk_ref[...] = (grad_product * v_ref[...].astype(F32)).astype(BF16)
    gv_ref[...] = (grad_product * k_ref[...].astype(F32)).astype(BF16)

    term_sum = terms[...]
    for d in range(1, n):
        term(d, ring(s - d)).wait_recv()
        term_sum = term_sum + terms_got[d - 1]
    gt_ref[...] = term_sum[0:TAPS, 0:GROUP]

    @pl.when(off_diagonal)
    def _():
        cross().wait_send()

    @pl.when(s < n - 1)
    def _():
        for copy in edges(s + 1):
            copy.wait_send()

    for h in range(2):
        for d in range(1, side):
            gather_a(h, d, 1).wait_send()
            for e in range(side):
                gather_b(h, d, e, 1).wait_send()

    def sent_hops(k, carry):
        for j in range(PARTS):
            for way in range(2):
                if way == last_way(j):
                    hop(way, k, j, z).wait_send()
                else:

                    @pl.when(k < far - 1)
                    def _():
                        hop(way, k, j, z).wait_send()

        return carry

    lax.fori_loop(0, far, sent_hops, 0)

    def sent_shares(t, carry):
        share(t, c).wait_send()
        return carry

    lax.fori_loop(0, n, sent_shares, 0)

    def sent_sums(outer, carry):
        for h in range(2):
            for d in range(1, side):
                one_copy(h, 0, outer, d, at_xy(y, x - 1)).wait_send()
        return carry

    lax.fori_loop(0, side, sent_sums, 0)
    for h in range(2):
        for d in range(1, side):
            two_copy(h, 0, d, at_xy(y, x - 1)).wait_send()

    @pl.when(s > 0)
    def _():
        back(s - 1).wait_send()

    for d in range(1, n):
        term(d, ring(s + d)).wait_send()


def shards(side, q, k, v, g, w, taps):
    n = side * side
    rows, chans = q.shape
    wide = chans // 2
    vmem = pl.BlockSpec(memory_space=pltpu.VMEM)
    dma = pltpu.SemaphoreType.DMA
    sems = [
        (1,), (1,), (1,), (2,), (2,),
        (2, side - 1), (2, side - 1), (2, side - 1, side), (2, side - 1, side),
        (2, n // 2, PARTS), (2, n // 2, PARTS), (n,), (n,),
        (2, side, side - 1), (2, side, side - 1), (2, side - 1), (2, side - 1),
        (1,), (1,), (n - 1,), (n - 1,), (5,),
    ]
    return pl.pallas_call(
        functools.partial(kernel, side),
        out_shape=(
            jax.ShapeDtypeStruct((rows, chans), BF16),
            jax.ShapeDtypeStruct((rows, chans), BF16),
            jax.ShapeDtypeStruct((rows, chans), BF16),
            jax.ShapeDtypeStruct(w.shape, F32),
            jax.ShapeDtypeStruct(taps.shape, F32),
        ),
        in_specs=[pl.BlockSpec(memory_space=pltpu.HBM)] * 6,
        out_specs=[vmem] * 5,
        scratch_shapes=[
            pltpu.VMEM((2, n, rows, chans), BF16),
            pltpu.VMEM((n, rows, chans), BF16),
            pltpu.VMEM((2, n, rows, wide), BF16),
            pltpu.VMEM((2, side, side - 1, rows, wide), BF16),
            pltpu.VMEM((2, side, rows, wide), F32),
            pltpu.VMEM((2, side, rows, wide), F32),
            pltpu.VMEM((2, side - 1, rows, wide), F32),
            pltpu.VMEM((2, rows, wide), F32),
            pltpu.VMEM((rows, chans), BF16),
            pltpu.VMEM((rows, chans), BF16),
            pltpu.VMEM((rows, chans), BF16),
            pltpu.VMEM(w.shape, BF16),
            pltpu.VMEM(taps.shape, F32),
            pltpu.VMEM((PAD, chans), BF16),
            pltpu.VMEM((PAD, chans), BF16),
            pltpu.VMEM((PAD + rows, chans), F32),
            pltpu.VMEM((rows, chans), F32),
            pltpu.VMEM((rows + EDGE, chans), F32),
            pltpu.VMEM((8, chans), F32),
            pltpu.VMEM((8, 128), F32),
            pltpu.VMEM((n - 1, 8, 128), F32),
        ]
        + [dma(shape) for shape in sems],
        compiler_params=pltpu.CompilerParams(
            collective_id=0, has_side_effects=True, vmem_limit_bytes=63 * 2**20
        ),
    )(q, k, v, g, w, taps)


def solution(mesh):
    side = int(round(mesh.shape["seq"] ** 0.5))
    tiles, weight, filters = P("seq", "mp"), P("mp", "seq"), P(None, "mp")
    return jax.shard_map(
        functools.partial(shards, side),
        mesh=mesh,
        in_specs=(tiles, tiles, tiles, tiles, weight, filters),
        out_specs=(tiles, tiles, tiles, weight, filters),
        check_vma=False,
    )
```

```python
import functools

import jax
import jax.numpy as jnp
from jax import lax
from jax.experimental import pallas as pl
from jax.experimental.pallas import tpu as pltpu
from jax.sharding import PartitionSpec as P

TAPS = 7
GROUP = 16
PAD = 16
EDGE = 8
PARTS = 4
MESH = pl.DeviceIdType.MESH
F32 = jnp.float32
BF16 = jnp.bfloat16


def dot(a, b, dims):
    return lax.dot_general(a, b, ((dims[0:1], dims[1:2]), ((), ())), preferred_element_type=F32)


def exact_dot(a, b):
    return lax.dot_general(
        a,
        b,
        (((1,), (0,)), ((), ())),
        precision=lax.Precision.HIGHEST,
        preferred_element_type=F32,
    )


def kernel(
    side,
    q_in, k_in, v_in, g_ref, w_in, taps_in,
    gq_ref, gk_ref, gv_ref, gw_ref, gt_ref,
    cols, gat, sent1, got1, own, sent2, got2, fin,
    q_ref, k_ref, v_ref, w_ref, taps_ref, k_edge, v_edge, prod, filt, gfil, spread, terms, terms_got,
    cross_s, cross_r, cross_l, edge_s, edge_r, ga_s, ga_r, gb_s, gb_r,
    ring_s, ring_r, core_s, core_r, one_s, one_r, two_s, two_r,
    back_s, back_r, term_s, term_r, load_s,
):
    n = side * side
    far = n // 2
    rows, chans = q_in.shape
    half, wide, slab = rows // 2, chans // 2, rows // PARTS
    s, m = lax.axis_index("seq"), lax.axis_index("mp")
    z, c = m // 2, m % 2
    y, x = s // side, s % side
    loads = [
        pltpu.make_async_copy(src, dst, load_s.at[i])
        for i, (src, dst) in enumerate(
            ((k_in, k_ref), (v_in, v_ref), (taps_in, taps_ref), (q_in, q_ref), (w_in, w_ref))
        )
    ]
    for load in loads:
        load.start()

    def ring(t):
        return lax.rem(t + 4 * n, n)

    def seq_dev(i):
        return (i, m)

    def at_xy(yy, xx):
        return (lax.rem(yy + side, side) * side + lax.rem(xx + side, side), m)

    def rc(src, dst, ss, rs, dev):
        return pltpu.make_async_remote_copy(
            src_ref=src, dst_ref=dst, send_sem=ss, recv_sem=rs, device_id=dev, device_id_type=MESH
        )


    def skew(i):
        return i + side * (i % side)

    target = ring(s + skew(z))
    crossed = (z, 2 * target + c)
    source = (ring(z - skew(s)), 2 * s + c)
    up, down = (s, 2 * ring(z + 1) + c), (s, 2 * ring(z - 1) + c)
    mate = (s, 2 * z + 1 - c)
    off_diagonal = jnp.logical_or(s != z, target != z)

    barrier = pltpu.get_barrier_semaphore()
    for d in range(1, n):
        pl.semaphore_signal(
            barrier, inc=1, device_id=seq_dev(ring(s + d)), device_id_type=MESH
        )
    for dev in (up, down, mate):
        pl.semaphore_signal(barrier, inc=1, device_id=dev, device_id_type=MESH)

    @pl.when(off_diagonal)
    def _():
        pl.semaphore_signal(barrier, inc=1, device_id=source, device_id_type=MESH)

    for load in loads:
        load.wait()
    group = lax.broadcasted_iota(jnp.int32, (GROUP, chans), 1) // GROUP
    lane = lax.broadcasted_iota(jnp.int32, (GROUP, chans), 0)
    spread[0:TAPS] = exact_dot(taps_ref[...], jnp.where(group == lane, 1.0, 0.0).astype(F32))
    prod[PAD:] = k_ref[...].astype(F32) * v_ref[...].astype(F32)

    total = jnp.zeros((rows - PAD, chans), F32)
    for o in range(TAPS):
        total = total + spread[o : o + 1] * prod[2 * PAD - o : PAD - o + rows]
    filt[PAD:] = total

    @pl.when(off_diagonal)
    def _():
        pl.semaphore_wait(barrier, n + 3)

    @pl.when(jnp.logical_not(off_diagonal))
    def _():
        pl.semaphore_wait(barrier, n + 2)

    def cross():
        return rc(g_ref, cols.at[c, target], cross_s.at[0], cross_r.at[0], crossed)

    def cross_in():
        return rc(g_ref, cols.at[c, z], cross_s.at[0], cross_r.at[0], crossed)

    def cross_local():
        return pltpu.make_async_copy(g_ref, cols.at[c, z], cross_l.at[0])

    @pl.when(off_diagonal)
    def _():
        cross().start()

    @pl.when(jnp.logical_not(off_diagonal))
    def _():
        cross_local().start()

    def edges(dev):
        tail = pl.ds(rows - PAD, PAD)
        return (
            rc(k_in.at[tail], k_edge, edge_s.at[0], edge_r.at[0], seq_dev(dev)),
            rc(v_in.at[tail], v_edge, edge_s.at[1], edge_r.at[1], seq_dev(dev)),
        )

    @pl.when(s < n - 1)
    def _():
        for copy in edges(s + 1):
            copy.start()


    @pl.when(s == 0)
    def _():
        prod[0:PAD] = jnp.zeros((PAD, chans), F32)

    @pl.when(s > 0)
    def _():
        for copy in edges(s - 1):
            copy.wait_recv()
        prod[0:PAD] = k_edge[...].astype(F32) * v_edge[...].astype(F32)

    first = jnp.zeros((PAD, chans), F32)
    for o in range(TAPS):
        first = first + spread[o : o + 1] * prod[PAD - o : 2 * PAD - o]
    filt[0:PAD] = first
    gated = (q_ref[...].astype(F32) * filt[...]).astype(BF16)
    gat[s] = gated

    def gather_a(h, d, sign):
        to = at_xy(y, x + d * sign) if h == 0 else at_xy(y + d * sign, x)
        block = s if sign > 0 else to[0]
        piece = gat.at[block, pl.ds(h * half, half)]
        return rc(piece, piece, ga_s.at[h, d - 1], ga_r.at[h, d - 1], to)

    def gather_b(h, d, e, sign):
        if h == 0:
            block, to = at_xy(y, x - e)[0], at_xy(y + d * sign, x)
            came = at_xy(y - d, x - e)[0]
        else:
            block, to = at_xy(y - e, x)[0], at_xy(y, x + d * sign)
            came = at_xy(y - e, x - d)[0]
        piece = gat.at[block if sign > 0 else came, pl.ds(h * half, half)]
        return rc(piece, piece, gb_s.at[h, d - 1, e], gb_r.at[h, d - 1, e], to)

    for d in range(1, side):
        for h in range(2):
            gather_a(h, d, 1).start()
    for h in range(2):
        for d in range(1, side):
            gather_b(h, d, 0, 1).start()
    for e in range(1, side):
        for h in range(2):
            gather_a(h, e, -1).wait_recv()
            for d in range(1, side):
                gather_b(h, d, e, 1).start()

    def hop(way, k, j, t):
        piece = cols.at[c, t, pl.ds(j * slab, slab)]
        sems = ring_s.at[way, k, j], ring_r.at[way, k, j]
        return rc(piece, piece, *sems, up if way == 0 else down)

    def share(t, which):
        piece = cols.at[which, t]
        return rc(piece, piece, core_s.at[t], core_r.at[t], mate)

    @pl.when(off_diagonal)
    def _():
        cross_in().wait_recv()

    @pl.when(jnp.logical_not(off_diagonal))
    def _():
        cross_local().wait()

    for j in range(PARTS):
        for way in range(2):
            hop(way, 0, j, z).start()
    share(z, c).start()

    def last_way(j):
        return 2 * j // PARTS

    def leg_one(h, t):
        ty, tx = t // side, t % side
        outer, inner, here = (ty, tx, x) if h == 0 else (tx, ty, y)
        d = lax.rem(inner - here + side, side)
        to = at_xy(y, tx) if h == 0 else at_xy(ty, x)
        return outer, d, to

    def one_copy(h, t, outer, d, to):
        return rc(
            sent1.at[h, t], got1.at[h, outer, d - 1],
            one_s.at[h, outer, d - 1], one_r.at[h, outer, d - 1], to,
        )

    def process(p):
        t = ring(p - skew(s))
        share(p, 1 - c).wait_recv()
        part = dot(cols[0, p], w_ref[:, :chans], (1, 1)) + dot(cols[1, p], w_ref[:, chans:], (1, 1))
        for h in range(2):
            outer, d, to = leg_one(h, t)
            piece = part[:, h * wide : (h + 1) * wide]

            @pl.when(d == 0)
            def _():
                own[h, outer] = piece

            @pl.when(d != 0)
            def _():
                sent1[h, t] = piece.astype(BF16)
                one_copy(h, t, outer, d, to).start()

    def two_copy(h, outer, d, to):
        return rc(
            sent2.at[h, outer], got2.at[h, d - 1], two_s.at[h, d - 1], two_r.at[h, d - 1], to
        )

    def step(k, carry):
        a, b = ring(z - k), ring(z + k)

        def pass_on(j):
            @pl.when(k < far)
            def _():
                for way, p in ((0, a), (1, b)):
                    hop(way, k - 1, j, p).wait_recv()
                    if way == last_way(j):
                        hop(way, k, j, p).start()
                    else:

                        @pl.when(k < far - 1)
                        def _():
                            hop(way, k, j, p).start()

            @pl.when(k == far)
            def _():
                hop(last_way(j), far - 1, j, a).wait_recv()

        for j in range(PARTS // 2):
            pass_on(j)
        process(ring(z - k + 1))
        for j in range(PARTS // 2, PARTS):
            pass_on(j)

        @pl.when(k <= far)
        def _():
            share(a, c).start()

        @pl.when(k < far)
        def _():
            share(b, c).start()

        @pl.when(jnp.logical_and(k > 1, k <= far))
        def _():
            process(ring(z + k - 1))

        return carry

    lax.fori_loop(1, far + 2, step, 0)

    for i in range(1, side + 1):
        d = i % side
        for h in range(2):
            outer = lax.rem((y if h == 0 else x) + i, side)
            acc = own[h, outer]
            for e in range(1, side):
                one_copy(h, 0, outer, e, at_xy(y, x - 1)).wait_recv()
                acc = acc + got1[h, outer, e - 1].astype(F32)
            if d:
                sent2[h, outer] = acc
                two_copy(h, outer, d, at_xy(y + d, x) if h == 0 else at_xy(y, x + d)).start()
            else:
                fin[h] = acc

    for h in range(2):
        for d in range(1, side):
            for e in range(side):
                gather_b(h, d, e, -1).wait_recv()
    gw_ref[...] = jnp.zeros(gw_ref.shape, F32)

    def weigh(p, carry):
        near = gat[ring(p - skew(s))]
        gw_ref[:, :chans] += dot(near, cols[0, p], (0, 0))
        gw_ref[:, chans:] += dot(near, cols[1, p], (0, 0))
        return carry

    lax.fori_loop(0, n, weigh, 0)

    for h in range(2):
        span = slice(h * wide, (h + 1) * wide)
        acc = fin[h]
        for d in range(1, side):
            two_copy(h, 0, d, at_xy(y, x - 1)).wait_recv()
            acc = acc + got2[h, d - 1]
        gq_ref[:, span] = (acc * filt[:, span]).astype(BF16)
        gfil[0:rows, span] = acc * q_ref[:, span].astype(F32)

    def back(dev):
        return rc(
            gfil.at[pl.ds(0, EDGE)], gfil.at[pl.ds(rows, EDGE)],
            back_s.at[0], back_r.at[0], seq_dev(dev),
        )

    @pl.when(s > 0)
    def _():
        back(s - 1).start()

    @pl.when(s == n - 1)
    def _():
        gfil[rows:] = jnp.zeros((EDGE, chans), F32)

    grad_filtered = gfil[0:rows]
    term_rows = [
        jnp.sum(grad_filtered * prod[PAD - o : PAD - o + rows], 0, keepdims=True)
        for o in range(TAPS)
    ]
    stacked = jnp.concatenate(term_rows + [jnp.zeros((1, chans), F32)], 0)
    lanes = terms.shape[1]
    group_t = lax.broadcasted_iota(jnp.int32, (chans, lanes), 0) // GROUP
    lane_t = lax.broadcasted_iota(jnp.int32, (chans, lanes), 1)
    terms[...] = exact_dot(stacked, jnp.where(group_t == lane_t, 1.0, 0.0).astype(F32))

    def term(d, dev):
        return rc(terms, terms_got.at[d - 1], term_s.at[d - 1], term_r.at[d - 1], seq_dev(dev))

    for d in range(1, n):
        term(d, ring(s + d)).start()

    @pl.when(s < n - 1)
    def _():
        back(s + 1).wait_recv()

    grad_product = jnp.zeros((rows, chans), F32)
    for o in range(TAPS):
        grad_product = grad_product + spread[o : o + 1] * gfil[o : o + rows]
    gk_ref[...] = (grad_product * v_ref[...].astype(F32)).astype(BF16)
    gv_ref[...] = (grad_product * k_ref[...].astype(F32)).astype(BF16)

    term_sum = terms[...]
    for d in range(1, n):
        term(d, ring(s - d)).wait_recv()
        term_sum = term_sum + terms_got[d - 1]
    gt_ref[...] = term_sum[0:TAPS, 0:GROUP]

    @pl.when(off_diagonal)
    def _():
        cross().wait_send()

    @pl.when(s < n - 1)
    def _():
        for copy in edges(s + 1):
            copy.wait_send()

    for h in range(2):
        for d in range(1, side):
            gather_a(h, d, 1).wait_send()
            for e in range(side):
                gather_b(h, d, e, 1).wait_send()

    def sent_hops(k, carry):
        for j in range(PARTS):
            for way in range(2):
                if way == last_way(j):
                    hop(way, k, j, z).wait_send()
                else:

                    @pl.when(k < far - 1)
                    def _():
                        hop(way, k, j, z).wait_send()

        return carry

    lax.fori_loop(0, far, sent_hops, 0)

    def sent_shares(t, carry):
        share(t, c).wait_send()
        return carry

    lax.fori_loop(0, n, sent_shares, 0)

    def sent_sums(outer, carry):
        for h in range(2):
            for d in range(1, side):
                one_copy(h, 0, outer, d, at_xy(y, x - 1)).wait_send()
        return carry

    lax.fori_loop(0, side, sent_sums, 0)
    for h in range(2):
        for d in range(1, side):
            two_copy(h, 0, d, at_xy(y, x - 1)).wait_send()

    @pl.when(s > 0)
    def _():
        back(s - 1).wait_send()

    for d in range(1, n):
        term(d, ring(s + d)).wait_send()


def write_out(*refs):
    results, outs, held, sems = refs[0:5], refs[5:10], refs[10:15], refs[15]
    loads = [pltpu.make_async_copy(results[i], held[i], sems.at[0, i]) for i in range(5)]
    stores = [pltpu.make_async_copy(held[i], outs[i], sems.at[1, i]) for i in range(5)]
    for load in loads:
        load.start()
    for load, store in zip(loads, stores):
        load.wait()
        store.start()
    for store in stores:
        store.wait()


def shards(side, q, k, v, g, w, taps):
    n = side * side
    rows, chans = q.shape
    wide = chans // 2
    vmem = pl.BlockSpec(memory_space=pltpu.VMEM)
    dma = pltpu.SemaphoreType.DMA
    sems = [
        (1,), (1,), (1,), (2,), (2,),
        (2, side - 1), (2, side - 1), (2, side - 1, side), (2, side - 1, side),
        (2, n // 2, PARTS), (2, n // 2, PARTS), (n,), (n,),
        (2, side, side - 1), (2, side, side - 1), (2, side - 1), (2, side - 1),
        (1,), (1,), (n - 1,), (n - 1,), (5,),
    ]
    results = pl.pallas_call(
        functools.partial(kernel, side),
        out_shape=(
            jax.ShapeDtypeStruct((rows, chans), BF16),
            jax.ShapeDtypeStruct((rows, chans), BF16),
            jax.ShapeDtypeStruct((rows, chans), BF16),
            jax.ShapeDtypeStruct(w.shape, F32),
            jax.ShapeDtypeStruct(taps.shape, F32),
        ),
        in_specs=[pl.BlockSpec(memory_space=pltpu.HBM)] * 6,
        out_specs=[vmem] * 5,
        scratch_shapes=[
            pltpu.VMEM((2, n, rows, chans), BF16),
            pltpu.VMEM((n, rows, chans), BF16),
            pltpu.VMEM((2, n, rows, wide), BF16),
            pltpu.VMEM((2, side, side - 1, rows, wide), BF16),
            pltpu.VMEM((2, side, rows, wide), F32),
            pltpu.VMEM((2, side, rows, wide), F32),
            pltpu.VMEM((2, side - 1, rows, wide), F32),
            pltpu.VMEM((2, rows, wide), F32),
            pltpu.VMEM((rows, chans), BF16),
            pltpu.VMEM((rows, chans), BF16),
            pltpu.VMEM((rows, chans), BF16),
            pltpu.VMEM(w.shape, BF16),
            pltpu.VMEM(taps.shape, F32),
            pltpu.VMEM((PAD, chans), BF16),
            pltpu.VMEM((PAD, chans), BF16),
            pltpu.VMEM((PAD + rows, chans), F32),
            pltpu.VMEM((rows, chans), F32),
            pltpu.VMEM((rows + EDGE, chans), F32),
            pltpu.VMEM((8, chans), F32),
            pltpu.VMEM((8, 128), F32),
            pltpu.VMEM((n - 1, 8, 128), F32),
        ]
        + [dma(shape) for shape in sems],
        compiler_params=pltpu.CompilerParams(
            collective_id=0, has_side_effects=True, vmem_limit_bytes=63 * 2**20
        ),
    )(q, k, v, g, w, taps)
    return pl.pallas_call(
        write_out,
        out_shape=tuple(jax.ShapeDtypeStruct(r.shape, r.dtype) for r in results),
        in_specs=[pl.BlockSpec(memory_space=pltpu.HBM)] * 5,
        out_specs=[pl.BlockSpec(memory_space=pltpu.HBM)] * 5,
        scratch_shapes=[pltpu.VMEM(r.shape, r.dtype) for r in results] + [dma((2, 5))],
        compiler_params=pltpu.CompilerParams(vmem_limit_bytes=63 * 2**20),
    )(*results)


def solution(mesh):
    side = int(round(mesh.shape["seq"] ** 0.5))
    tiles, weight, filters = P("seq", "mp"), P("mp", "seq"), P(None, "mp")
    return jax.shard_map(
        functools.partial(shards, side),
        mesh=mesh,
        in_specs=(tiles, tiles, tiles, tiles, weight, filters),
        out_specs=(tiles, tiles, tiles, weight, filters),
        check_vma=False,
    )
```

```python
import functools

import jax
import jax.numpy as jnp
from jax import lax
from jax.experimental import pallas as pl
from jax.experimental.pallas import tpu as pltpu
from jax.sharding import PartitionSpec as P

TAPS = 7
GROUP = 16
PAD = 16
EDGE = 8
PARTS = 4
MESH = pl.DeviceIdType.MESH
F32 = jnp.float32
BF16 = jnp.bfloat16


def dot(a, b, dims):
    return lax.dot_general(a, b, ((dims[0:1], dims[1:2]), ((), ())), preferred_element_type=F32)


def exact_dot(a, b):
    return lax.dot_general(
        a,
        b,
        (((1,), (0,)), ((), ())),
        precision=lax.Precision.HIGHEST,
        preferred_element_type=F32,
    )


def kernel(
    side,
    q_in, k_in, v_in, g_ref, w_in, taps_in,
    gq_ref, gk_ref, gv_ref, gw_ref, gt_ref,
    cols, gat, sent1, got1, own, sent2, got2, fin,
    q_ref, k_ref, v_ref, w_ref, taps_ref, k_edge, v_edge, prod, filt, gfil, spread, terms, terms_got,
    cross_s, cross_r, cross_l, edge_s, edge_r, ga_s, ga_r, gb_s, gb_r,
    ring_s, ring_r, core_s, core_r, one_s, one_r, two_s, two_r,
    back_s, back_r, term_s, term_r, load_s,
):
    n = side * side
    far = n // 2
    rows, chans = q_in.shape
    half, wide, slab = rows // 2, chans // 2, rows // PARTS
    s, m = lax.axis_index("seq"), lax.axis_index("mp")
    z, c = m // 2, m % 2
    y, x = s // side, s % side
    loads = [
        pltpu.make_async_copy(src, dst, load_s.at[i])
        for i, (src, dst) in enumerate(
            ((k_in, k_ref), (v_in, v_ref), (taps_in, taps_ref), (q_in, q_ref), (w_in, w_ref))
        )
    ]
    for load in loads:
        load.start()

    def ring(t):
        return lax.rem(t + 4 * n, n)

    def seq_dev(i):
        return (i, m)

    def at_xy(yy, xx):
        return (lax.rem(yy + side, side) * side + lax.rem(xx + side, side), m)

    def rc(src, dst, ss, rs, dev):
        return pltpu.make_async_remote_copy(
            src_ref=src, dst_ref=dst, send_sem=ss, recv_sem=rs, device_id=dev, device_id_type=MESH
        )


    def skew(i):
        return i + side * (i % side)

    target = ring(s + skew(z))
    crossed = (z, 2 * target + c)
    source = (ring(z - skew(s)), 2 * s + c)
    up, down = (s, 2 * ring(z + 1) + c), (s, 2 * ring(z - 1) + c)
    mate = (s, 2 * z + 1 - c)
    off_diagonal = jnp.logical_or(s != z, target != z)

    barrier = pltpu.get_barrier_semaphore()
    for d in range(1, n):
        pl.semaphore_signal(
            barrier, inc=1, device_id=seq_dev(ring(s + d)), device_id_type=MESH
        )
    for dev in (up, down, mate):
        pl.semaphore_signal(barrier, inc=1, device_id=dev, device_id_type=MESH)

    @pl.when(off_diagonal)
    def _():
        pl.semaphore_signal(barrier, inc=1, device_id=source, device_id_type=MESH)

    for load in loads:
        load.wait()
    group = lax.broadcasted_iota(jnp.int32, (GROUP, chans), 1) // GROUP
    lane = lax.broadcasted_iota(jnp.int32, (GROUP, chans), 0)
    spread[0:TAPS] = exact_dot(taps_ref[...], jnp.where(group == lane, 1.0, 0.0).astype(F32))
    prod[PAD:] = k_ref[...].astype(F32) * v_ref[...].astype(F32)

    total = jnp.zeros((rows - PAD, chans), F32)
    for o in range(TAPS):
        total = total + spread[o : o + 1] * prod[2 * PAD - o : PAD - o + rows]
    filt[PAD:] = total

    @pl.when(off_diagonal)
    def _():
        pl.semaphore_wait(barrier, n + 3)

    @pl.when(jnp.logical_not(off_diagonal))
    def _():
        pl.semaphore_wait(barrier, n + 2)

    def cross():
        return rc(g_ref, cols.at[c, target], cross_s.at[0], cross_r.at[0], crossed)

    def cross_in():
        return rc(g_ref, cols.at[c, z], cross_s.at[0], cross_r.at[0], crossed)

    def cross_local():
        return pltpu.make_async_copy(g_ref, cols.at[c, z], cross_l.at[0])

    @pl.when(off_diagonal)
    def _():
        cross().start()

    @pl.when(jnp.logical_not(off_diagonal))
    def _():
        cross_local().start()

    def edges(dev):
        tail = pl.ds(rows - PAD, PAD)
        return (
            rc(k_in.at[tail], k_edge, edge_s.at[0], edge_r.at[0], seq_dev(dev)),
            rc(v_in.at[tail], v_edge, edge_s.at[1], edge_r.at[1], seq_dev(dev)),
        )

    @pl.when(s < n - 1)
    def _():
        for copy in edges(s + 1):
            copy.start()


    @pl.when(s == 0)
    def _():
        prod[0:PAD] = jnp.zeros((PAD, chans), F32)

    @pl.when(s > 0)
    def _():
        for copy in edges(s - 1):
            copy.wait_recv()
        prod[0:PAD] = k_edge[...].astype(F32) * v_edge[...].astype(F32)

    first = jnp.zeros((PAD, chans), F32)
    for o in range(TAPS):
        first = first + spread[o : o + 1] * prod[PAD - o : 2 * PAD - o]
    filt[0:PAD] = first
    gated = (q_ref[...].astype(F32) * filt[...]).astype(BF16)
    gat[s] = gated

    def gather_a(h, d, sign):
        to = at_xy(y, x + d * sign) if h == 0 else at_xy(y + d * sign, x)
        block = s if sign > 0 else to[0]
        piece = gat.at[block, pl.ds(h * half, half)]
        return rc(piece, piece, ga_s.at[h, d - 1], ga_r.at[h, d - 1], to)

    def gather_b(h, d, e, sign):
        if h == 0:
            block, to = at_xy(y, x - e)[0], at_xy(y + d * sign, x)
            came = at_xy(y - d, x - e)[0]
        else:
            block, to = at_xy(y - e, x)[0], at_xy(y, x + d * sign)
            came = at_xy(y - e, x - d)[0]
        piece = gat.at[block if sign > 0 else came, pl.ds(h * half, half)]
        return rc(piece, piece, gb_s.at[h, d - 1, e], gb_r.at[h, d - 1, e], to)

    for d in range(1, side):
        for h in range(2):
            gather_a(h, d, 1).start()
    for h in range(2):
        for d in range(1, side):
            gather_b(h, d, 0, 1).start()
    for e in range(1, side):
        for h in range(2):
            gather_a(h, e, -1).wait_recv()
            for d in range(1, side):
                gather_b(h, d, e, 1).start()

    def hop(way, k, j, t):
        piece = cols.at[c, t, pl.ds(j * slab, slab)]
        sems = ring_s.at[way, k, j], ring_r.at[way, k, j]
        return rc(piece, piece, *sems, up if way == 0 else down)

    def share(t, which):
        piece = cols.at[which, t]
        return rc(piece, piece, core_s.at[t], core_r.at[t], mate)

    @pl.when(off_diagonal)
    def _():
        cross_in().wait_recv()

    @pl.when(jnp.logical_not(off_diagonal))
    def _():
        cross_local().wait()

    for j in range(PARTS):
        for way in range(2):
            hop(way, 0, j, z).start()
    share(z, c).start()

    def last_way(j):
        return 2 * j // PARTS

    def leg_one(h, t):
        ty, tx = t // side, t % side
        outer, inner, here = (ty, tx, x) if h == 0 else (tx, ty, y)
        d = lax.rem(inner - here + side, side)
        to = at_xy(y, tx) if h == 0 else at_xy(ty, x)
        return outer, d, to

    def one_copy(h, t, outer, d, to):
        return rc(
            sent1.at[h, t], got1.at[h, outer, d - 1],
            one_s.at[h, outer, d - 1], one_r.at[h, outer, d - 1], to,
        )

    def process(p):
        t = ring(p - skew(s))
        share(p, 1 - c).wait_recv()
        part = dot(cols[0, p], w_ref[:, :chans], (1, 1)) + dot(cols[1, p], w_ref[:, chans:], (1, 1))
        for h in range(2):
            outer, d, to = leg_one(h, t)
            piece = part[:, h * wide : (h + 1) * wide]

            @pl.when(d == 0)
            def _():
                own[h, outer] = piece

            @pl.when(d != 0)
            def _():
                sent1[h, t] = piece.astype(BF16)
                one_copy(h, t, outer, d, to).start()

    def two_copy(h, outer, d, to):
        return rc(
            sent2.at[h, outer], got2.at[h, d - 1], two_s.at[h, d - 1], two_r.at[h, d - 1], to
        )

    def step(k, carry):
        a, b = ring(z - k), ring(z + k)

        def pass_on(j):
            @pl.when(k < far)
            def _():
                for way, p in ((0, a), (1, b)):
                    hop(way, k - 1, j, p).wait_recv()
                    if way == last_way(j):
                        hop(way, k, j, p).start()
                    else:

                        @pl.when(k < far - 1)
                        def _():
                            hop(way, k, j, p).start()

            @pl.when(k == far)
            def _():
                hop(last_way(j), far - 1, j, a).wait_recv()

        for j in range(PARTS // 2):
            pass_on(j)
        process(ring(z - k + 1))
        for j in range(PARTS // 2, PARTS):
            pass_on(j)

        @pl.when(k <= far)
        def _():
            share(a, c).start()

        @pl.when(k < far)
        def _():
            share(b, c).start()

        @pl.when(jnp.logical_and(k > 1, k <= far))
        def _():
            process(ring(z + k - 1))

        return carry

    lax.fori_loop(1, far + 2, step, 0)

    for i in range(1, side + 1):
        d = i % side
        for h in range(2):
            outer = lax.rem((y if h == 0 else x) + i, side)
            acc = own[h, outer]
            for e in range(1, side):
                one_copy(h, 0, outer, e, at_xy(y, x - 1)).wait_recv()
                acc = acc + got1[h, outer, e - 1].astype(F32)
            if d:
                sent2[h, outer] = acc
                two_copy(h, outer, d, at_xy(y + d, x) if h == 0 else at_xy(y, x + d)).start()
            else:
                fin[h] = acc

    for h in range(2):
        for d in range(1, side):
            for e in range(side):
                gather_b(h, d, e, -1).wait_recv()
    gw_ref[...] = jnp.zeros(gw_ref.shape, F32)

    def weigh(p, carry):
        near = gat[ring(p - skew(s))]
        gw_ref[:, :chans] += dot(near, cols[0, p], (0, 0))
        gw_ref[:, chans:] += dot(near, cols[1, p], (0, 0))
        return carry

    lax.fori_loop(0, n, weigh, 0)

    for h in range(2):
        span = slice(h * wide, (h + 1) * wide)
        acc = fin[h]
        for d in range(1, side):
            two_copy(h, 0, d, at_xy(y, x - 1)).wait_recv()
            acc = acc + got2[h, d - 1]
        fin[h] = acc
        gfil[0:rows, span] = acc * q_ref[:, span].astype(F32)

    def back(dev):
        return rc(
            gfil.at[pl.ds(0, EDGE)], gfil.at[pl.ds(rows, EDGE)],
            back_s.at[0], back_r.at[0], seq_dev(dev),
        )

    @pl.when(s > 0)
    def _():
        back(s - 1).start()

    @pl.when(s == n - 1)
    def _():
        gfil[rows:] = jnp.zeros((EDGE, chans), F32)

    grad_filtered = gfil[0:rows]
    term_rows = [
        jnp.sum(grad_filtered * prod[PAD - o : PAD - o + rows], 0, keepdims=True)
        for o in range(TAPS)
    ]
    stacked = jnp.concatenate(term_rows + [jnp.zeros((1, chans), F32)], 0)
    lanes = terms.shape[1]
    group_t = lax.broadcasted_iota(jnp.int32, (chans, lanes), 0) // GROUP
    lane_t = lax.broadcasted_iota(jnp.int32, (chans, lanes), 1)
    terms[...] = exact_dot(stacked, jnp.where(group_t == lane_t, 1.0, 0.0).astype(F32))

    def term(d, dev):
        return rc(terms, terms_got.at[d - 1], term_s.at[d - 1], term_r.at[d - 1], seq_dev(dev))

    for d in range(1, n):
        term(d, ring(s + d)).start()

    for h in range(2):
        span = slice(h * wide, (h + 1) * wide)
        gq_ref[:, span] = (fin[h] * filt[:, span]).astype(BF16)

    @pl.when(s < n - 1)
    def _():
        back(s + 1).wait_recv()

    grad_product = jnp.zeros((rows, chans), F32)
    for o in range(TAPS):
        grad_product = grad_product + spread[o : o + 1] * gfil[o : o + rows]
    gk_ref[...] = (grad_product * v_ref[...].astype(F32)).astype(BF16)
    gv_ref[...] = (grad_product * k_ref[...].astype(F32)).astype(BF16)

    term_sum = terms[...]
    for d in range(1, n):
        term(d, ring(s - d)).wait_recv()
        term_sum = term_sum + terms_got[d - 1]
    gt_ref[...] = term_sum[0:TAPS, 0:GROUP]

    @pl.when(off_diagonal)
    def _():
        cross().wait_send()

    @pl.when(s < n - 1)
    def _():
        for copy in edges(s + 1):
            copy.wait_send()

    for h in range(2):
        for d in range(1, side):
            gather_a(h, d, 1).wait_send()
            for e in range(side):
                gather_b(h, d, e, 1).wait_send()

    def sent_hops(k, carry):
        for j in range(PARTS):
            for way in range(2):
                if way == last_way(j):
                    hop(way, k, j, z).wait_send()
                else:

                    @pl.when(k < far - 1)
                    def _():
                        hop(way, k, j, z).wait_send()

        return carry

    lax.fori_loop(0, far, sent_hops, 0)

    def sent_shares(t, carry):
        share(t, c).wait_send()
        return carry

    lax.fori_loop(0, n, sent_shares, 0)

    def sent_sums(outer, carry):
        for h in range(2):
            for d in range(1, side):
                one_copy(h, 0, outer, d, at_xy(y, x - 1)).wait_send()
        return carry

    lax.fori_loop(0, side, sent_sums, 0)
    for h in range(2):
        for d in range(1, side):
            two_copy(h, 0, d, at_xy(y, x - 1)).wait_send()

    @pl.when(s > 0)
    def _():
        back(s - 1).wait_send()

    for d in range(1, n):
        term(d, ring(s + d)).wait_send()


def write_out(*refs):
    results, outs, held, sems = refs[0:5], refs[5:10], refs[10:15], refs[15]
    loads = [pltpu.make_async_copy(results[i], held[i], sems.at[0, i]) for i in range(5)]
    stores = [pltpu.make_async_copy(held[i], outs[i], sems.at[1, i]) for i in range(5)]
    for load in loads:
        load.start()
    for load, store in zip(loads, stores):
        load.wait()
        store.start()
    for store in stores:
        store.wait()


def shards(side, q, k, v, g, w, taps):
    n = side * side
    rows, chans = q.shape
    wide = chans // 2
    vmem = pl.BlockSpec(memory_space=pltpu.VMEM)
    dma = pltpu.SemaphoreType.DMA
    sems = [
        (1,), (1,), (1,), (2,), (2,),
        (2, side - 1), (2, side - 1), (2, side - 1, side), (2, side - 1, side),
        (2, n // 2, PARTS), (2, n // 2, PARTS), (n,), (n,),
        (2, side, side - 1), (2, side, side - 1), (2, side - 1), (2, side - 1),
        (1,), (1,), (n - 1,), (n - 1,), (5,),
    ]
    results = pl.pallas_call(
        functools.partial(kernel, side),
        out_shape=(
            jax.ShapeDtypeStruct((rows, chans), BF16),
            jax.ShapeDtypeStruct((rows, chans), BF16),
            jax.ShapeDtypeStruct((rows, chans), BF16),
            jax.ShapeDtypeStruct(w.shape, F32),
            jax.ShapeDtypeStruct(taps.shape, F32),
        ),
        in_specs=[pl.BlockSpec(memory_space=pltpu.HBM)] * 6,
        out_specs=[vmem] * 5,
        scratch_shapes=[
            pltpu.VMEM((2, n, rows, chans), BF16),
            pltpu.VMEM((n, rows, chans), BF16),
            pltpu.VMEM((2, n, rows, wide), BF16),
            pltpu.VMEM((2, side, side - 1, rows, wide), BF16),
            pltpu.VMEM((2, side, rows, wide), F32),
            pltpu.VMEM((2, side, rows, wide), F32),
            pltpu.VMEM((2, side - 1, rows, wide), F32),
            pltpu.VMEM((2, rows, wide), F32),
            pltpu.VMEM((rows, chans), BF16),
            pltpu.VMEM((rows, chans), BF16),
            pltpu.VMEM((rows, chans), BF16),
            pltpu.VMEM(w.shape, BF16),
            pltpu.VMEM(taps.shape, F32),
            pltpu.VMEM((PAD, chans), BF16),
            pltpu.VMEM((PAD, chans), BF16),
            pltpu.VMEM((PAD + rows, chans), F32),
            pltpu.VMEM((rows, chans), F32),
            pltpu.VMEM((rows + EDGE, chans), F32),
            pltpu.VMEM((8, chans), F32),
            pltpu.VMEM((8, 128), F32),
            pltpu.VMEM((n - 1, 8, 128), F32),
        ]
        + [dma(shape) for shape in sems],
        compiler_params=pltpu.CompilerParams(
            collective_id=0, has_side_effects=True, vmem_limit_bytes=63 * 2**20
        ),
    )(q, k, v, g, w, taps)
    return pl.pallas_call(
        write_out,
        out_shape=tuple(jax.ShapeDtypeStruct(r.shape, r.dtype) for r in results),
        in_specs=[pl.BlockSpec(memory_space=pltpu.HBM)] * 5,
        out_specs=[pl.BlockSpec(memory_space=pltpu.HBM)] * 5,
        scratch_shapes=[pltpu.VMEM(r.shape, r.dtype) for r in results] + [dma((2, 5))],
        compiler_params=pltpu.CompilerParams(vmem_limit_bytes=63 * 2**20),
    )(*results)


def solution(mesh):
    side = int(round(mesh.shape["seq"] ** 0.5))
    tiles, weight, filters = P("seq", "mp"), P("mp", "seq"), P(None, "mp")
    return jax.shard_map(
        functools.partial(shards, side),
        mesh=mesh,
        in_specs=(tiles, tiles, tiles, tiles, weight, filters),
        out_specs=(tiles, tiles, tiles, weight, filters),
        check_vma=False,
    )
```
